32 devices in a mesh: walk: 4 (over x, core), pb: 8 (over z, y).
Axes of the slice: x: 2, y: 2, z: 4, core: 2. Of those that a mesh axis runs over, the one named last changes fastest.
Arguments:
- greens: bfloat16 [64, 64, 3072], P('walk', 'pb'), may hold values from -6 to 6
- cholesky: bfloat16 [32, 300, 3072], P('pb'), may hold values from -0.011962891 to 0.011962891
- slot_source: int32 [32], replicated, may hold values from 0 to 63, as said below
- block_transfer_index: int32 [32], P('pb'), may hold values from 0 to 15
- slot_multiplicity: int32 [32], P('pb'), may hold values from 0 to 3, as said below
- fields: float32 [64, 16, 300], P('walk'), may hold values from -6 to 6
- weight: float32 [64], P('walk'), may hold values from 0.2 to 5
Outputs:
- force_bias: float32 [64, 2, 4800], P('walk', None, 'pb')
- local_energy: float32 [64], P('walk')
- new_weight: float32 [64], P('walk')
- mixed_energy: float32 [], replicated
The draws below stay inside these ranges and needn't reach their ends.
Inputs may be any that keep to these rules, and one draw needn't show every extreme that they name: `slot_source`: the Green's block of k-point k lies on index k // 8 of pb; with P = 8, slot j of pb index d (slot d * 4 + j) reads a block that lies on index (d + o_j) mod P of pb, where o_0 = 0, o_1 = P - 1, o_2 = 1, o_3 = P // 2. `slot_multiplicity`: 0 marks an empty slot; on each index of pb the live slots come first, and on some index all 4 slots are live.
All inputs are finite; a program needn't handle non-finite values.
Results may differ from the reference program's by a relative error of at most 0.0003.
Values may be sent and summed in bfloat16 or wider, within the bound.
A program may use at most 320 MiB of HBM per device.

```python
import math
import jax
import jax.numpy as jnp
from jax import lax

K = 64
ORBITAL_COUNT = 96
OCCUPIED_COUNT = 16
CHOLESKY_COUNT = 300
TRANSFER_COUNT = 16
PAIR_BLOCKS_HELD = 4
NW = 64
KPOINTS_PER_PART = 8
PAIR_BLOCK_TOTAL = 32


def draw_slot_source(key, part):
    group_list = PAIR_BLOCK_TOTAL // PAIR_BLOCKS_HELD
    offsets = jnp.array([0, group_list - 1, 1, group_list // 2], dtype=jnp.int32)
    owner_parts = (jnp.arange(group_list, dtype=jnp.int32)[:, None] + offsets[None, :]) % group_list
    within_group = jax.random.randint(jax.random.fold_in(key, 12), (group_list, PAIR_BLOCKS_HELD), 0, KPOINTS_PER_PART)
    return (owner_parts * KPOINTS_PER_PART + within_group).reshape(PAIR_BLOCK_TOTAL).astype(jnp.int32)


def draw_slot_multiplicity(key, part):
    group_list = PAIR_BLOCK_TOTAL // PAIR_BLOCKS_HELD
    first_draw = jax.random.randint(jax.random.fold_in(key, 21), (group_list,), 0, PAIR_BLOCKS_HELD)
    second_draw = jax.random.randint(jax.random.fold_in(key, 22), (group_list,), 0, PAIR_BLOCKS_HELD)
    live_count = 1 + first_draw * second_draw // max(PAIR_BLOCKS_HELD - 1, 1)
    full_index = jax.random.randint(jax.random.fold_in(key, 23), (), 0, group_list)
    live_count = jnp.where(jnp.arange(group_list) == full_index, PAIR_BLOCKS_HELD, live_count)
    levels = jax.random.randint(jax.random.fold_in(key, 24), (group_list, PAIR_BLOCKS_HELD), 1, 4)
    corner = (jnp.arange(group_list)[:, None] == full_index) & (jnp.arange(PAIR_BLOCKS_HELD)[None, :] == 0)
    levels = jnp.where(corner, 3, levels)
    multiple_count = jnp.where(jnp.arange(PAIR_BLOCKS_HELD)[None, :] < live_count[:, None], levels, 0)
    return multiple_count.reshape(PAIR_BLOCK_TOTAL).astype(jnp.int32)


def touch_ends(values, rng, least, largest):
    index_at = [jax.random.randint(jax.random.fold_in(rng, axis), (), 0, length) for axis, length in enumerate(values.shape)]
    longest = values.shape.index(max(values.shape))
    neighbour = index_at[:longest] + [(index_at[longest] + 1) % values.shape[longest]] + index_at[longest + 1:]
    return values.at[tuple(index_at)].set(least).at[tuple(neighbour)].set(largest)


def block_levels(stream_key, extent, split, low, high):
    def one(dim, shards_of):
        draws = jax.random.uniform(jax.random.fold_in(jax.random.fold_in(stream_key, 6), dim), (shards_of,), jnp.float32, low / len(split), high / len(split))
        return jnp.repeat(jnp.exp(draws), extent[dim] // shards_of).reshape((-1,) + (1,) * (len(extent) - dim - 1))

    gain = one(*split[0])
    for cut in split[1:]:
        gain = gain * one(*cut)
    return gain


def bell_draw(own_key, dims, spread, bound, cuts=(), held_as=jnp.bfloat16):
    level = block_levels(own_key, dims, cuts, -0.22, 0.18) if cuts else 1.0
    entries = jax.random.normal(own_key, dims, jnp.float32) * spread * level
    return jnp.minimum(jnp.maximum(entries, -bound), bound).astype(held_as)


def setup_inputs(seed: int = 0) -> dict:
    key_list = jax.random.split(jax.random.key(seed), 8)
    greens = bell_draw(key_list[0], (NW, K, OCCUPIED_COUNT * 2 * ORBITAL_COUNT), 1.0, 6.0, ((0, 4), (1, 8)))
    cholesky = bell_draw(key_list[1], (PAIR_BLOCK_TOTAL, CHOLESKY_COUNT, OCCUPIED_COUNT * 2 * ORBITAL_COUNT), 0.002, 0.011962891, ((0, 8),))
    slot_source = draw_slot_source(jax.random.fold_in(key_list[7], 71), 0)
    block_transfer_index = touch_ends(jax.random.randint(key_list[3], (PAIR_BLOCK_TOTAL,), 0, TRANSFER_COUNT), jax.random.fold_in(key_list[3], 1), 0, TRANSFER_COUNT - 1).astype(jnp.int32)
    slot_multiplicity = draw_slot_multiplicity(jax.random.fold_in(key_list[7], 71), 0)
    fields = bell_draw(key_list[5], (NW, TRANSFER_COUNT, CHOLESKY_COUNT), 1.0, 6.0, ((0, 4),), jnp.float32)
    weight = jnp.clip(jnp.exp(math.log(5.0) - 3.218876 * jax.random.uniform(key_list[6], (NW,), jnp.float32) ** block_levels(key_list[6], (NW,), ((0, 4),), -0.2, 0.2)), 0.2, 5.0)
    return dict(greens=greens, cholesky=cholesky, slot_source=slot_source, block_transfer_index=block_transfer_index, slot_multiplicity=slot_multiplicity, fields=fields, weight=weight)


sqrt_step = 0.05

def slot_terms(chol_flat, green_flat):
    vectors = chol_flat.shape[0]
    walkers = green_flat.shape[0]
    doubled = 2 * ORBITAL_COUNT
    chol_block = chol_flat.reshape(vectors, OCCUPIED_COUNT, doubled)
    green_rows = green_flat.reshape(walkers, OCCUPIED_COUNT, doubled)
    real_part = green_rows[..., :ORBITAL_COUNT]
    imag_part = green_rows[..., ORBITAL_COUNT:]
    stacked = jnp.stack([jnp.concatenate([real_part, -imag_part], -1), jnp.concatenate([imag_part, real_part], -1)], 0)
    left_matrix = chol_block.reshape(vectors * OCCUPIED_COUNT, doubled)
    right_matrix = stacked.reshape(2 * walkers * OCCUPIED_COUNT, doubled)
    product = jnp.dot(left_matrix, right_matrix.T, preferred_element_type=jnp.float32)
    product = product.reshape(vectors, OCCUPIED_COUNT, 2, walkers, OCCUPIED_COUNT)
    identity = jnp.eye(OCCUPIED_COUNT, dtype=jnp.float32)
    diagonal = jnp.einsum('nicwj,ij->wcn', product, identity)
    crossed = jnp.einsum('nicwj,njcwi->cw', product, product)
    return (diagonal, crossed[0] - crossed[1])

def reference(greens, cholesky, slot_source, block_transfer_index, slot_multiplicity, fields, weight):

    def advance(running, inputs):
        bias, exchange_sum = running
        chol_block, source, transfer, multiple_count = inputs
        green_rows = lax.dynamic_index_in_dim(greens, source.astype(jnp.int32), 1, keepdims=False)
        diagonal, crossed = slot_terms(chol_block, green_rows)
        scaled = multiple_count.astype(jnp.float32)
        factor = scaled * (jnp.arange(TRANSFER_COUNT) == transfer).astype(jnp.float32)
        bias = bias + factor[None, None, :, None] * diagonal[:, :, None, :]
        exchange_sum = exchange_sum + scaled * crossed
        return ((bias, exchange_sum), None)
    initial = (jnp.zeros((NW, 2, TRANSFER_COUNT, CHOLESKY_COUNT), jnp.float32), jnp.zeros((NW,), jnp.float32))
    (bias, exchange_sum), unused = lax.scan(advance, initial, (cholesky, slot_source, block_transfer_index, slot_multiplicity))
    bias = bias.reshape(NW, 2, TRANSFER_COUNT * CHOLESKY_COUNT)
    real_bias = bias[:, 0]
    imag_bias = bias[:, 1]
    flat_fields = fields.reshape(NW, TRANSFER_COUNT * CHOLESKY_COUNT)
    coulomb = 0.5 * lax.optimization_barrier(jnp.sum(real_bias * real_bias - imag_bias * imag_bias, axis=1))
    energy = coulomb - 0.5 * exchange_sum
    shift_real = sqrt_step * real_bias
    shift_imag = sqrt_step * imag_bias
    real_arg = lax.optimization_barrier(jnp.sum(flat_fields * shift_real - 0.5 * (shift_real * shift_real - shift_imag * shift_imag), axis=1))
    imag_arg = lax.optimization_barrier(jnp.sum(flat_fields * shift_imag - shift_real * shift_imag, axis=1))
    new_weight = weight * jnp.exp(real_arg) * jnp.maximum(jnp.cos(imag_arg), 0.0)
    mixed = jnp.sum(weight * energy) / jnp.sum(weight)
    return (bias, energy, new_weight, mixed)
```

```python
import functools

import jax
import jax.numpy as jnp
import numpy as np
from jax import lax
from jax.experimental import pallas as pl
from jax.experimental.pallas import tpu as pltpu
from jax.sharding import PartitionSpec as P

ORBITAL_COUNT = 96
OCCUPIED_COUNT = 16
TRANSFER_COUNT = 16
SQRT_STEP = 0.05

DOUBLED = 2 * ORBITAL_COUNT
PAIR = 2 * DOUBLED
WINDOW = 256
SHIFT = PAIR - WINDOW
VMEM_LIMIT = 60 * 1024 * 1024
F32 = jnp.float32


def offsets_of(devices):
    return [0, devices - 1, 1, devices // 2]


def arrangement():
    table = np.zeros((2, WINDOW, 2, 2, WINDOW), np.float32)
    for parity in range(2):
        start = parity * (DOUBLED - SHIFT)
        for window in range(2):
            out = window * (DOUBLED - SHIFT)
            for q in range(ORBITAL_COUNT):
                re, im = start + q, start + ORBITAL_COUNT + q
                first, second = out + q, out + ORBITAL_COUNT + q
                table[parity, re, window, 0, first] = 1.0
                table[parity, im, window, 0, second] = -1.0
                table[parity, im, window, 1, first] = 1.0
                table[parity, re, window, 1, second] = 1.0
    return table.reshape(2, WINDOW, 4 * WINDOW)


def select_kernel(devices, source_ref, greens_ref, out_ref, wide, picked):
    me = lax.axis_index("pb")
    walkers, kpoints, _ = greens_ref.shape
    slots = out_ref.shape[0]
    for w in range(walkers):
        wide[w] = greens_ref[w].astype(F32)
    for slot in range(slots):
        requester = lax.rem(me + devices - offsets_of(devices)[slot], devices)
        index = lax.rem(source_ref[requester * slots + slot], kpoints)
        for w in range(walkers):
            picked[slot, w : w + 1, :] = wide[w, pl.ds(index, 1), :]
        out_ref[slot] = picked[slot].astype(out_ref.dtype)


def exchange_kernel(devices, mine_ref, out_ref, landed, send_sems, recv_sems):
    me = lax.axis_index("pb")
    slots = mine_ref.shape[0]
    offsets = offsets_of(devices)
    barrier = pltpu.get_barrier_semaphore()
    for slot in range(1, slots):
        pl.semaphore_signal(
            barrier,
            inc=1,
            device_id={"pb": lax.rem(me + devices - offsets[slot], devices)},
            device_id_type=pl.DeviceIdType.MESH,
        )
    pl.semaphore_wait(barrier, slots - 1)
    copies = []
    for slot in range(slots - 1, 0, -1):
        copy = pltpu.make_async_remote_copy(
            src_ref=mine_ref.at[slot],
            dst_ref=landed.at[slot - 1],
            send_sem=send_sems.at[slot - 1],
            recv_sem=recv_sems.at[slot - 1],
            device_id={"pb": lax.rem(me + devices - offsets[slot], devices)},
            device_id_type=pl.DeviceIdType.MESH,
        )
        copy.start()
        copies.append((slot, copy))
    out_ref[0] = mine_ref[0]
    for slot, copy in reversed(copies):
        copy.wait_recv()
        out_ref[slot] = landed[slot - 1]
    for slot, copy in copies:
        copy.wait_send()


def row_of(part, occupied, walkers):
    half = (OCCUPIED_COUNT // 2) * walkers
    return part * 2 * half + (occupied % 2) * half + (occupied // 2) * walkers


def compute_kernel(
    transfer_ref, multiple_ref, green_ref, chol_ref, table_ref, dense_ref, cross_ref, operand, product, diagonal, crossed
):
    slot = pl.program_id(0)
    slots = pl.num_programs(0)
    walkers = green_ref.shape[1]
    vectors = chol_ref.shape[1]
    half = (OCCUPIED_COUNT // 2) * walkers
    pairs = OCCUPIED_COUNT // 2
    scaled = multiple_ref[slot].astype(F32)

    for parity in range(2):
        rows = jnp.concatenate(
            [green_ref[0, :, PAIR * p + SHIFT * parity : PAIR * p + SHIFT * parity + WINDOW] for p in range(pairs)], 0
        )
        spread = jnp.dot(rows, table_ref[parity], preferred_element_type=F32).astype(operand.dtype)
        for window in range(2):
            for part in range(2):
                at = (window * 2 + part) * WINDOW
                operand[window, pl.ds(part * 2 * half + parity * half, half), :] = spread[:, at : at + WINDOW]

    for i in range(OCCUPIED_COUNT):
        start = PAIR * (i // 2) + SHIFT * (i % 2)
        product[i] = lax.dot_general(
            operand[i % 2],
            chol_ref[0, :, start : start + WINDOW],
            (((1,), (1,)), ((), ())),
            preferred_element_type=F32,
        )

    def block(i, j, part):
        return product[i, pl.ds(row_of(part, j, walkers), walkers), :]

    zero = jnp.zeros((walkers, vectors), F32)
    off = [zero, zero]
    own = [zero, zero]
    trace = [zero, zero]
    for i in range(OCCUPIED_COUNT):
        for part in range(2):
            here = block(i, i, part)
            own[part] = own[part] + here * here
            trace[part] = trace[part] + here
            for j in range(i):
                off[part] = off[part] + block(i, j, part) * block(j, i, part)
    for part in range(2):
        diagonal[slot, part] = scaled * trace[part]
    total = scaled * ((own[0] - own[1]) + 2.0 * (off[0] - off[1]))

    @pl.when(slot == 0)
    def _():
        crossed[...] = total

    @pl.when(slot > 0)
    def _():
        crossed[...] += total

    @pl.when(slot == slots - 1)
    def _():
        held = diagonal.shape[0]
        cross_ref[...] = jnp.sum(crossed[...], axis=1, keepdims=True)
        shares, _, _, width = dense_ref.shape
        for t in range(TRANSFER_COUNT):
            keep = [(transfer_ref[s] == t).astype(jnp.int32).astype(F32) for s in range(held)]
            for part in range(2):
                value = keep[0] * diagonal[0, part]
                for s in range(1, held):
                    value = value + keep[s] * diagonal[s, part]
                low, high = t * vectors, (t + 1) * vectors
                for share in range(low // width, (high - 1) // width + 1):
                    first, last = max(low, share * width), min(high, (share + 1) * width)
                    dense_ref[share, part, :, first - share * width : last - share * width] = value[
                        :, first - low : last - low
                    ]


def reduce_kernel(
    devices,
    groups,
    dense_ref,
    cross_ref,
    field_ref,
    weight_ref,
    bias_ref,
    energy_ref,
    new_ref,
    mixed_ref,
    landed,
    own_sums,
    other_sums,
    own_mean,
    other_mean,
    share_send,
    share_recv,
    sum_send,
    sum_recv,
    mean_send,
    mean_recv,
):
    me = lax.axis_index("pb")
    group = lax.axis_index("walk")
    walkers = weight_ref.shape[1]

    def pb_peer(step):
        return {"pb": lax.rem(me + step, devices)}

    def walk_peer(step):
        return {"walk": lax.rem(group + step, groups)}

    barrier = pltpu.get_barrier_semaphore()
    for step in range(1, devices):
        pl.semaphore_signal(barrier, inc=1, device_id=pb_peer(step), device_id_type=pl.DeviceIdType.MESH)
    for step in range(1, groups):
        pl.semaphore_signal(barrier, inc=1, device_id=walk_peer(step), device_id_type=pl.DeviceIdType.MESH)
    pl.semaphore_wait(barrier, devices + groups - 2)

    def send_all(source_of, target, send_sems, recv_sems, peer, count):
        copies = []
        for step in range(1, count):
            copy = pltpu.make_async_remote_copy(
                src_ref=source_of(step),
                dst_ref=target.at[step - 1],
                send_sem=send_sems.at[step - 1],
                recv_sem=recv_sems.at[step - 1],
                device_id=peer(step),
                device_id_type=pl.DeviceIdType.MESH,
            )
            copy.start()
            copies.append(copy)
        return copies

    shares = send_all(
        lambda step: dense_ref.at[lax.rem(me + step, devices)], landed, share_send, share_recv, pb_peer, devices
    )
    row = lax.broadcasted_iota(jnp.int32, (walkers, walkers), 0)
    column = lax.broadcasted_iota(jnp.int32, (walkers, walkers), 1)
    same = row == column
    weight = jnp.sum(jnp.where(same, jnp.broadcast_to(weight_ref[...], (walkers, walkers)), 0.0), axis=1, keepdims=True)
    real, imag = dense_ref[me, 0], dense_ref[me, 1]
    for step in range(1, devices):
        shares[step - 1].wait_recv()
        real = real + landed[step - 1, 0]
        imag = imag + landed[step - 1, 1]
    bias_ref[:, 0, :] = real
    bias_ref[:, 1, :] = imag
    shift_real = SQRT_STEP * real
    shift_imag = SQRT_STEP * imag
    field = field_ref[...]
    coulomb = 0.5 * jnp.sum(real * real - imag * imag, axis=1, keepdims=True)
    real_arg = jnp.sum(
        field * shift_real - 0.5 * (shift_real * shift_real - shift_imag * shift_imag), axis=1, keepdims=True
    )
    imag_arg = jnp.sum(field * shift_imag - shift_real * shift_imag, axis=1, keepdims=True)
    lane = lax.broadcasted_iota(jnp.int32, own_sums.shape, 1)
    energy_part = coulomb - 0.5 * cross_ref[...]
    packed = jnp.where(lane == 0, energy_part, jnp.where(lane == 1, real_arg, jnp.where(lane == 2, imag_arg, 0.0)))
    own_sums[...] = packed
    sums = send_all(lambda step: own_sums, other_sums, sum_send, sum_recv, pb_peer, devices)
    for step in range(1, devices):
        sums[step - 1].wait_recv()
    total = jnp.zeros_like(packed)
    for index in range(devices):
        step = lax.rem(me + devices - index, devices)
        arrived = other_sums[jnp.maximum(step - 1, 0)]
        total = total + jnp.where(step == 0, packed, arrived)
    energy = jnp.sum(jnp.where(lane == 0, total, 0.0), axis=1, keepdims=True)
    full_real = jnp.sum(jnp.where(lane == 1, total, 0.0), axis=1, keepdims=True)
    full_imag = jnp.sum(jnp.where(lane == 2, total, 0.0), axis=1, keepdims=True)
    weighted = jnp.sum(weight * energy, axis=0, keepdims=True)
    weights = jnp.sum(weight, axis=0, keepdims=True)
    lane = lax.broadcasted_iota(jnp.int32, own_mean.shape, 1)
    mean = jnp.where(lane == 0, weighted, jnp.where(lane == 1, weights, 0.0))
    own_mean[...] = mean
    means = send_all(lambda step: own_mean, other_mean, mean_send, mean_recv, walk_peer, groups)
    new_weight = weight * jnp.exp(full_real) * jnp.maximum(jnp.cos(full_imag), 0.0)
    energy_ref[...] = jnp.sum(jnp.where(same, energy, 0.0), axis=0, keepdims=True)
    new_ref[...] = jnp.sum(jnp.where(same, new_weight, 0.0), axis=0, keepdims=True)
    for step in range(1, groups):
        means[step - 1].wait_recv()
    total = jnp.zeros_like(mean)
    for index in range(groups):
        step = lax.rem(group + groups - index, groups)
        arrived = other_mean[jnp.maximum(step - 1, 0)]
        total = total + jnp.where(step == 0, mean, arrived)
    upper = jnp.sum(jnp.where(lane == 0, total, 0.0)[:1], axis=1, keepdims=True)
    lower = jnp.sum(jnp.where(lane == 1, total, 0.0)[:1], axis=1, keepdims=True)
    mixed_ref[...] = upper / lower
    for copy in shares + sums + means:
        copy.wait_send()


def local(greens, cholesky, slot_source, block_transfer_index, slot_multiplicity, fields, weight):
    devices = lax.axis_size("pb")
    groups = lax.axis_size("walk")
    me = lax.axis_index("pb")
    walkers, kpoints, flat = greens.shape
    slots, vectors, _ = cholesky.shape
    width = TRANSFER_COUNT * vectors // devices
    vmem = pl.BlockSpec(memory_space=pltpu.VMEM)
    smem = pl.BlockSpec(memory_space=pltpu.SMEM)

    outgoing = pl.pallas_call(
        functools.partial(select_kernel, devices),
        out_shape=jax.ShapeDtypeStruct((slots, walkers, flat), greens.dtype),
        in_specs=[smem, vmem],
        out_specs=vmem,
        scratch_shapes=[pltpu.VMEM((walkers, kpoints, flat), F32), pltpu.VMEM((slots, walkers, flat), F32)],
        compiler_params=pltpu.CompilerParams(vmem_limit_bytes=VMEM_LIMIT),
        name="select",
    )(slot_source, greens)

    blocks = pl.pallas_call(
        functools.partial(exchange_kernel, devices),
        out_shape=jax.ShapeDtypeStruct((slots, walkers, flat), greens.dtype),
        in_specs=[vmem],
        out_specs=vmem,
        scratch_shapes=[
            pltpu.VMEM((slots - 1, walkers, flat), greens.dtype),
            pltpu.SemaphoreType.DMA((slots - 1,)),
            pltpu.SemaphoreType.DMA((slots - 1,)),
        ],
        compiler_params=pltpu.CompilerParams(collective_id=0, has_side_effects=True),
        name="exchange",
    )(outgoing)

    rows = 2 * OCCUPIED_COUNT * walkers
    dense, cross = pl.pallas_call(
        compute_kernel,
        grid=(slots,),
        out_shape=(
            jax.ShapeDtypeStruct((devices, 2, walkers, width), F32),
            jax.ShapeDtypeStruct((walkers, 1), F32),
        ),
        in_specs=[
            smem,
            smem,
            pl.BlockSpec((1, walkers, flat), lambda s: (s, 0, 0)),
            pl.BlockSpec((1, vectors, flat), lambda s: (s, 0, 0)),
            pl.BlockSpec((2, WINDOW, 4 * WINDOW), lambda s: (0, 0, 0)),
        ],
        out_specs=(
            pl.BlockSpec((devices, 2, walkers, width), lambda s: (0, 0, 0, 0)),
            pl.BlockSpec((walkers, 1), lambda s: (0, 0)),
        ),
        scratch_shapes=[
            pltpu.VMEM((2, rows, WINDOW), greens.dtype),
            pltpu.VMEM((OCCUPIED_COUNT, rows, vectors), F32),
            pltpu.VMEM((slots, 2, walkers, vectors), F32),
            pltpu.VMEM((walkers, vectors), F32),
        ],
        compiler_params=pltpu.CompilerParams(
            dimension_semantics=("arbitrary",), vmem_limit_bytes=VMEM_LIMIT
        ),
        name="terms",
    )(block_transfer_index, slot_multiplicity, blocks, cholesky, jnp.asarray(arrangement(), greens.dtype))

    if width % vectors == 0:
        each = width // vectors
        field_share = lax.dynamic_slice_in_dim(fields, me * each, each, 1).reshape(walkers, width)
    else:
        flat_fields = fields.reshape(walkers, TRANSFER_COUNT * vectors)
        field_share = lax.dynamic_slice_in_dim(flat_fields, me * width, width, 1)

    bias, energy, new_weight, mixed = pl.pallas_call(
        functools.partial(reduce_kernel, devices, groups),
        out_shape=(
            jax.ShapeDtypeStruct((walkers, 2, width), F32),
            jax.ShapeDtypeStruct((1, walkers), F32),
            jax.ShapeDtypeStruct((1, walkers), F32),
            jax.ShapeDtypeStruct((1, 1), F32),
        ),
        in_specs=[vmem] * 4,
        out_specs=(vmem,) * 4,
        scratch_shapes=[
            pltpu.VMEM((devices - 1, 2, walkers, width), F32),
            pltpu.VMEM((walkers, 128), F32),
            pltpu.VMEM((devices - 1, walkers, 128), F32),
            pltpu.VMEM((8, 128), F32),
            pltpu.VMEM((groups - 1, 8, 128), F32),
            pltpu.SemaphoreType.DMA((devices - 1,)),
            pltpu.SemaphoreType.DMA((devices - 1,)),
            pltpu.SemaphoreType.DMA((devices - 1,)),
            pltpu.SemaphoreType.DMA((devices - 1,)),
            pltpu.SemaphoreType.DMA((groups - 1,)),
            pltpu.SemaphoreType.DMA((groups - 1,)),
        ],
        compiler_params=pltpu.CompilerParams(collective_id=1, has_side_effects=True, vmem_limit_bytes=VMEM_LIMIT),
        name="reduce",
    )(dense, cross, field_share, weight.reshape(1, walkers))
    return (bias, energy.reshape(walkers), new_weight.reshape(walkers), mixed.reshape(()))


def solution(mesh):
    placed = (
        P("walk", "pb", None),
        P("pb", None, None),
        P(),
        P("pb"),
        P("pb"),
        P("walk", None, None),
        P("walk"),
    )
    return jax.shard_map(
        local,
        mesh=mesh,
        in_specs=placed,
        out_specs=(P("walk", None, "pb"), P("walk"), P("walk"), P()),
        check_vma=False,
    )
```

```python
import functools

import jax
import jax.numpy as jnp
import numpy as np
from jax import lax
from jax.experimental import pallas as pl
from jax.experimental.pallas import tpu as pltpu
from jax.sharding import PartitionSpec as P

ORBITAL_COUNT = 96
OCCUPIED_COUNT = 16
TRANSFER_COUNT = 16
SQRT_STEP = 0.05

DOUBLED = 2 * ORBITAL_COUNT
PAIR = 2 * DOUBLED
WINDOW = 256
SHIFT = PAIR - WINDOW
VMEM_LIMIT = 60 * 1024 * 1024
F32 = jnp.float32


def offsets_of(devices):
    return [0, devices - 1, 1, devices // 2]


def arrangement():
    table = np.zeros((2, WINDOW, 2, 2, WINDOW), np.float32)
    for parity in range(2):
        start = parity * (DOUBLED - SHIFT)
        for window in range(2):
            out = window * (DOUBLED - SHIFT)
            for q in range(ORBITAL_COUNT):
                re, im = start + q, start + ORBITAL_COUNT + q
                first, second = out + q, out + ORBITAL_COUNT + q
                table[parity, re, window, 0, first] = 1.0
                table[parity, im, window, 0, second] = -1.0
                table[parity, im, window, 1, first] = 1.0
                table[parity, re, window, 1, second] = 1.0
    return table.reshape(2, WINDOW, 4 * WINDOW)


def select_kernel(devices, source_ref, greens_ref, *rest):
    me = lax.axis_index("pb")
    walkers, kpoints, _ = greens_ref.shape
    outs, (wide, picked) = rest[:-2], rest[-2:]
    slots = len(outs)
    for w in range(walkers):
        wide[w] = greens_ref[w].astype(F32)
    for slot in range(slots):
        requester = lax.rem(me + devices - offsets_of(devices)[slot], devices)
        index = lax.rem(source_ref[requester * slots + slot], kpoints)
        for w in range(walkers):
            picked[slot, w : w + 1, :] = wide[w, pl.ds(index, 1), :]
        outs[slot][...] = picked[slot].astype(greens_ref.dtype)


def row_of(part, occupied, walkers):
    half = (OCCUPIED_COUNT // 2) * walkers
    return part * 2 * half + (occupied % 2) * half + (occupied // 2) * walkers


def compute_kernel(
    transfer_ref, multiple_ref, chol_ref, table_ref, *rest
):
    greens, (dense_ref, cross_ref, operand, product, diagonal, crossed, green) = rest[:-7], rest[-7:]
    slot = pl.program_id(0)
    slots = pl.num_programs(0)
    walkers = green.shape[0]
    vectors = chol_ref.shape[1]
    half = (OCCUPIED_COUNT // 2) * walkers
    pairs = OCCUPIED_COUNT // 2
    scaled = multiple_ref[slot].astype(F32)

    for index, green_ref in enumerate(greens):

        @pl.when(slot == index)
        def _():
            green[...] = green_ref[...]


    for parity in range(2):
        rows = jnp.concatenate(
            [green[:, PAIR * p + SHIFT * parity : PAIR * p + SHIFT * parity + WINDOW] for p in range(pairs)], 0
        )
        spread = jnp.dot(rows, table_ref[parity], preferred_element_type=F32).astype(operand.dtype)
        for window in range(2):
            for part in range(2):
                at = (window * 2 + part) * WINDOW
                operand[window, pl.ds(part * 2 * half + parity * half, half), :] = spread[:, at : at + WINDOW]

    for i in range(OCCUPIED_COUNT):
        start = PAIR * (i // 2) + SHIFT * (i % 2)
        product[i] = lax.dot_general(
            operand[i % 2],
            chol_ref[0, :, start : start + WINDOW],
            (((1,), (1,)), ((), ())),
            preferred_element_type=F32,
        )

    def block(i, j, part):
        return product[i, pl.ds(row_of(part, j, walkers), walkers), :]

    zero = jnp.zeros((walkers, vectors), F32)
    off = [zero, zero]
    own = [zero, zero]
    trace = [zero, zero]
    for i in range(OCCUPIED_COUNT):
        for part in range(2):
            here = block(i, i, part)
            own[part] = own[part] + here * here
            trace[part] = trace[part] + here
            for j in range(i):
                off[part] = off[part] + block(i, j, part) * block(j, i, part)
    for part in range(2):
        diagonal[slot, part] = scaled * trace[part]
    total = scaled * ((own[0] - own[1]) + 2.0 * (off[0] - off[1]))

    @pl.when(slot == 0)
    def _():
        crossed[...] = total

    @pl.when(slot > 0)
    def _():
        crossed[...] += total

    @pl.when(slot == slots - 1)
    def _():
        held = diagonal.shape[0]
        cross_ref[...] = jnp.sum(crossed[...], axis=1, keepdims=True)
        shares, _, _, width = dense_ref.shape
        for t in range(TRANSFER_COUNT):
            keep = [(transfer_ref[s] == t).astype(jnp.int32).astype(F32) for s in range(held)]
            for part in range(2):
                value = keep[0] * diagonal[0, part]
                for s in range(1, held):
                    value = value + keep[s] * diagonal[s, part]
                low, high = t * vectors, (t + 1) * vectors
                for share in range(low // width, (high - 1) // width + 1):
                    first, last = max(low, share * width), min(high, (share + 1) * width)
                    dense_ref[share, part, :, first - share * width : last - share * width] = value[
                        :, first - low : last - low
                    ]


def on_diagonal(count):
    return lax.broadcasted_iota(jnp.int32, (count, count), 0) == lax.broadcasted_iota(jnp.int32, (count, count), 1)


def column_of(row):
    count = row.shape[1]
    return jnp.sum(jnp.where(on_diagonal(count), jnp.broadcast_to(row, (count, count)), 0.0), axis=1, keepdims=True)


def row_from(column):
    count = column.shape[0]
    return jnp.sum(jnp.where(on_diagonal(count), jnp.broadcast_to(column, (count, count)), 0.0), axis=0, keepdims=True)


def reduce_kernel(
    devices,
    groups,
    dense_ref,
    cross_ref,
    field_ref,
    weight_ref,
    bias_ref,
    total_ref,
    mean_ref,
    landed,
    own_sums,
    other_sums,
    own_mean,
    other_mean,
    share_send,
    share_recv,
    sum_send,
    sum_recv,
    mean_send,
    mean_recv,
):
    me = lax.axis_index("pb")
    group = lax.axis_index("walk")
    walkers = weight_ref.shape[1]

    def pb_peer(step):
        return {"pb": lax.rem(me + step, devices)}

    def walk_peer(step):
        return {"walk": lax.rem(group + step, groups)}

    barrier = pltpu.get_barrier_semaphore()
    for step in range(1, devices):
        pl.semaphore_signal(barrier, inc=1, device_id=pb_peer(step), device_id_type=pl.DeviceIdType.MESH)
    for step in range(1, groups):
        pl.semaphore_signal(barrier, inc=1, device_id=walk_peer(step), device_id_type=pl.DeviceIdType.MESH)
    pl.semaphore_wait(barrier, devices + groups - 2)

    def send_all(source_of, target, send_sems, recv_sems, peer, count):
        copies = []
        for step in range(1, count):
            copy = pltpu.make_async_remote_copy(
                src_ref=source_of(step),
                dst_ref=target.at[step - 1],
                send_sem=send_sems.at[step - 1],
                recv_sem=recv_sems.at[step - 1],
                device_id=peer(step),
                device_id_type=pl.DeviceIdType.MESH,
            )
            copy.start()
            copies.append(copy)
        return copies

    shares = send_all(
        lambda step: dense_ref.at[lax.rem(me + step, devices)], landed, share_send, share_recv, pb_peer, devices
    )
    weight = column_of(weight_ref[...])
    real, imag = dense_ref[me, 0], dense_ref[me, 1]
    for step in range(1, devices):
        shares[step - 1].wait_recv()
        real = real + landed[step - 1, 0]
        imag = imag + landed[step - 1, 1]
    bias_ref[0] = real
    bias_ref[1] = imag
    shift_real = SQRT_STEP * real
    shift_imag = SQRT_STEP * imag
    field = field_ref[...]
    coulomb = 0.5 * jnp.sum(real * real - imag * imag, axis=1, keepdims=True)
    real_arg = jnp.sum(
        field * shift_real - 0.5 * (shift_real * shift_real - shift_imag * shift_imag), axis=1, keepdims=True
    )
    imag_arg = jnp.sum(field * shift_imag - shift_real * shift_imag, axis=1, keepdims=True)
    lane = lax.broadcasted_iota(jnp.int32, own_sums.shape, 1)
    energy_part = coulomb - 0.5 * cross_ref[...]
    packed = jnp.where(lane == 0, energy_part, jnp.where(lane == 1, real_arg, jnp.where(lane == 2, imag_arg, 0.0)))
    own_sums[...] = packed
    sums = send_all(lambda step: own_sums, other_sums, sum_send, sum_recv, pb_peer, devices)
    for step in range(1, devices):
        sums[step - 1].wait_recv()
    total = jnp.zeros_like(packed)
    for index in range(devices):
        step = lax.rem(me + devices - index, devices)
        arrived = other_sums[jnp.maximum(step - 1, 0)]
        total = total + jnp.where(step == 0, packed, arrived)
    total_ref[...] = total
    energy = jnp.sum(jnp.where(lane == 0, total, 0.0), axis=1, keepdims=True)
    weighted = jnp.sum(weight * energy, axis=0, keepdims=True)
    weights = jnp.sum(weight, axis=0, keepdims=True)
    lane = lax.broadcasted_iota(jnp.int32, own_mean.shape, 1)
    mean = jnp.where(lane == 0, weighted, jnp.where(lane == 1, weights, 0.0))
    own_mean[...] = mean
    means = send_all(lambda step: own_mean, other_mean, mean_send, mean_recv, walk_peer, groups)
    for step in range(1, groups):
        means[step - 1].wait_recv()
    total = jnp.zeros_like(mean)
    for index in range(groups):
        step = lax.rem(group + groups - index, groups)
        arrived = other_mean[jnp.maximum(step - 1, 0)]
        total = total + jnp.where(step == 0, mean, arrived)
    mean_ref[...] = total
    for copy in shares + sums + means:
        copy.wait_send()


def finish_kernel(sums_ref, total_ref, mean_ref, weight_ref, bias_ref, energy_ref, new_ref, mixed_ref):
    bias_ref[:, 0, :] = sums_ref[0]
    bias_ref[:, 1, :] = sums_ref[1]
    total = total_ref[...]
    weight = column_of(weight_ref[...])
    lane = lax.broadcasted_iota(jnp.int32, total.shape, 1)
    energy = jnp.sum(jnp.where(lane == 0, total, 0.0), axis=1, keepdims=True)
    real = jnp.sum(jnp.where(lane == 1, total, 0.0), axis=1, keepdims=True)
    imag = jnp.sum(jnp.where(lane == 2, total, 0.0), axis=1, keepdims=True)
    energy_ref[...] = row_from(energy)
    new_ref[...] = row_from(weight * jnp.exp(real) * jnp.maximum(jnp.cos(imag), 0.0))
    mean = mean_ref[:1, :]
    mixed_ref[...] = mean[:, 0:1] / mean[:, 1:2]


def local(greens, cholesky, slot_source, block_transfer_index, slot_multiplicity, fields, weight):
    devices = lax.axis_size("pb")
    groups = lax.axis_size("walk")
    me = lax.axis_index("pb")
    walkers, kpoints, flat = greens.shape
    slots, vectors, _ = cholesky.shape
    width = TRANSFER_COUNT * vectors // devices
    vmem = pl.BlockSpec(memory_space=pltpu.VMEM)
    smem = pl.BlockSpec(memory_space=pltpu.SMEM)

    outgoing = pl.pallas_call(
        functools.partial(select_kernel, devices),
        out_shape=(jax.ShapeDtypeStruct((walkers, flat), greens.dtype),) * slots,
        in_specs=[smem, vmem],
        out_specs=(vmem,) * slots,
        scratch_shapes=[pltpu.VMEM((walkers, kpoints, flat), F32), pltpu.VMEM((slots, walkers, flat), F32)],
        compiler_params=pltpu.CompilerParams(vmem_limit_bytes=VMEM_LIMIT),
        name="select",
    )(slot_source, greens)

    arrived = [outgoing[0]]
    for slot in range(1, slots):
        by = devices - offsets_of(devices)[slot]
        arrived.append(lax.ppermute(outgoing[slot], "pb", [(i, (i + by) % devices) for i in range(devices)]))

    rows = 2 * OCCUPIED_COUNT * walkers
    dense, cross = pl.pallas_call(
        compute_kernel,
        grid=(slots,),
        out_shape=(
            jax.ShapeDtypeStruct((devices, 2, walkers, width), F32),
            jax.ShapeDtypeStruct((walkers, 1), F32),
        ),
        in_specs=[
            smem,
            smem,
            pl.BlockSpec((1, vectors, flat), lambda s: (s, 0, 0)),
            pl.BlockSpec((2, WINDOW, 4 * WINDOW), lambda s: (0, 0, 0)),
        ]
        + [pl.BlockSpec((walkers, flat), lambda s: (0, 0))] * slots,
        out_specs=(
            pl.BlockSpec((devices, 2, walkers, width), lambda s: (0, 0, 0, 0)),
            pl.BlockSpec((walkers, 1), lambda s: (0, 0)),
        ),
        scratch_shapes=[
            pltpu.VMEM((2, rows, WINDOW), greens.dtype),
            pltpu.VMEM((OCCUPIED_COUNT, rows, vectors), F32),
            pltpu.VMEM((slots, 2, walkers, vectors), F32),
            pltpu.VMEM((walkers, vectors), F32),
            pltpu.VMEM((walkers, flat), greens.dtype),
        ],
        compiler_params=pltpu.CompilerParams(
            dimension_semantics=("arbitrary",), vmem_limit_bytes=VMEM_LIMIT
        ),
        name="terms",
    )(block_transfer_index, slot_multiplicity, cholesky, jnp.asarray(arrangement(), greens.dtype), *arrived)

    if width % vectors == 0:
        each = width // vectors
        field_share = lax.dynamic_slice_in_dim(fields, me * each, each, 1).reshape(walkers, width)
    else:
        flat_fields = fields.reshape(walkers, TRANSFER_COUNT * vectors)
        field_share = lax.dynamic_slice_in_dim(flat_fields, me * width, width, 1)

    sums, total, mean = pl.pallas_call(
        functools.partial(reduce_kernel, devices, groups),
        out_shape=(
            jax.ShapeDtypeStruct((2, walkers, width), F32),
            jax.ShapeDtypeStruct((walkers, 128), F32),
            jax.ShapeDtypeStruct((8, 128), F32),
        ),
        in_specs=[vmem] * 4,
        out_specs=(vmem,) * 3,
        scratch_shapes=[
            pltpu.VMEM((devices - 1, 2, walkers, width), F32),
            pltpu.VMEM((walkers, 128), F32),
            pltpu.VMEM((devices - 1, walkers, 128), F32),
            pltpu.VMEM((8, 128), F32),
            pltpu.VMEM((groups - 1, 8, 128), F32),
            pltpu.SemaphoreType.DMA((devices - 1,)),
            pltpu.SemaphoreType.DMA((devices - 1,)),
            pltpu.SemaphoreType.DMA((devices - 1,)),
            pltpu.SemaphoreType.DMA((devices - 1,)),
            pltpu.SemaphoreType.DMA((groups - 1,)),
            pltpu.SemaphoreType.DMA((groups - 1,)),
        ],
        compiler_params=pltpu.CompilerParams(collective_id=1, has_side_effects=True, vmem_limit_bytes=VMEM_LIMIT),
        name="reduce",
    )(dense, cross, field_share, weight.reshape(1, walkers))

    bias, energy, new_weight, mixed = pl.pallas_call(
        finish_kernel,
        out_shape=(
            jax.ShapeDtypeStruct((walkers, 2, width), F32),
            jax.ShapeDtypeStruct((1, walkers), F32),
            jax.ShapeDtypeStruct((1, walkers), F32),
            jax.ShapeDtypeStruct((1, 1), F32),
        ),
        in_specs=[vmem] * 4,
        out_specs=(vmem,) * 4,
        name="finish",
    )(sums, total, mean, weight.reshape(1, walkers))
    return (bias, energy.reshape(walkers), new_weight.reshape(walkers), mixed.reshape(()))


def solution(mesh):
    placed = (
        P("walk", "pb", None),
        P("pb", None, None),
        P(),
        P("pb"),
        P("pb"),
        P("walk", None, None),
        P("walk"),
    )
    return jax.shard_map(
        local,
        mesh=mesh,
        in_specs=placed,
        out_specs=(P("walk", None, "pb"), P("walk"), P("walk"), P()),
        check_vma=False,
    )
```

```python
import functools

import jax
import jax.numpy as jnp
import numpy as np
from jax import lax
from jax.experimental import pallas as pl
from jax.experimental.pallas import tpu as pltpu
from jax.sharding import PartitionSpec as P

ORBITAL_COUNT = 96
OCCUPIED_COUNT = 16
TRANSFER_COUNT = 16
SQRT_STEP = 0.05

DOUBLED = 2 * ORBITAL_COUNT
PAIR = 2 * DOUBLED
WINDOW = 256
SHIFT = PAIR - WINDOW
VMEM_LIMIT = 60 * 1024 * 1024
F32 = jnp.float32


def offsets_of(devices):
    return [0, devices - 1, 1, devices // 2]


def arrangement():
    table = np.zeros((2, WINDOW, 2, 2, WINDOW), np.float32)
    for parity in range(2):
        start = parity * (DOUBLED - SHIFT)
        for window in range(2):
            out = window * (DOUBLED - SHIFT)
            for q in range(ORBITAL_COUNT):
                re, im = start + q, start + ORBITAL_COUNT + q
                first, second = out + q, out + ORBITAL_COUNT + q
                table[parity, re, window, 0, first] = 1.0
                table[parity, im, window, 0, second] = -1.0
                table[parity, im, window, 1, first] = 1.0
                table[parity, re, window, 1, second] = 1.0
    return table.reshape(2, WINDOW, 4 * WINDOW)


def select_kernel(devices, source_ref, greens_ref, *rest):
    me = lax.axis_index("pb")
    walkers, kpoints, _ = greens_ref.shape
    outs, (wide, picked) = rest[:-2], rest[-2:]
    slots = len(outs)
    for w in range(walkers):
        wide[w] = greens_ref[w].astype(F32)
    for slot in range(slots):
        requester = lax.rem(me + devices - offsets_of(devices)[slot], devices)
        index = lax.rem(source_ref[requester * slots + slot], kpoints)
        for w in range(walkers):
            picked[slot, w : w + 1, :] = wide[w, pl.ds(index, 1), :]
        outs[slot][...] = picked[slot].astype(greens_ref.dtype)


def row_of(part, occupied, walkers):
    half = (OCCUPIED_COUNT // 2) * walkers
    return part * 2 * half + (occupied % 2) * half + (occupied // 2) * walkers


def compute_kernel(
    transfer_ref, multiple_ref, chol_ref, table_ref, *rest
):
    greens, (dense_ref, cross_ref, operand, product, diagonal, crossed, green) = rest[:-7], rest[-7:]
    slot = pl.program_id(0)
    slots = pl.num_programs(0)
    walkers = green.shape[0]
    vectors = chol_ref.shape[1]
    half = (OCCUPIED_COUNT // 2) * walkers
    pairs = OCCUPIED_COUNT // 2
    scaled = multiple_ref[slot].astype(F32)

    for index, green_ref in enumerate(greens):

        @pl.when(slot == index)
        def _():
            green[...] = green_ref[...]


    for parity in range(2):
        rows = jnp.concatenate(
            [green[:, PAIR * p + SHIFT * parity : PAIR * p + SHIFT * parity + WINDOW] for p in range(pairs)], 0
        )
        spread = jnp.dot(rows, table_ref[parity], preferred_element_type=F32).astype(operand.dtype)
        for window in range(2):
            for part in range(2):
                at = (window * 2 + part) * WINDOW
                operand[window, pl.ds(part * 2 * half + parity * half, half), :] = spread[:, at : at + WINDOW]

    for i in range(OCCUPIED_COUNT):
        start = PAIR * (i // 2) + SHIFT * (i % 2)
        product[i] = lax.dot_general(
            operand[i % 2],
            chol_ref[0, :, start : start + WINDOW],
            (((1,), (1,)), ((), ())),
            preferred_element_type=F32,
        )

    def block(i, j, part):
        return product[i, pl.ds(row_of(part, j, walkers), walkers), :]

    zero = jnp.zeros((walkers, vectors), F32)
    off = [zero, zero]
    own = [zero, zero]
    trace = [zero, zero]
    for i in range(OCCUPIED_COUNT):
        for part in range(2):
            here = block(i, i, part)
            own[part] = own[part] + here * here
            trace[part] = trace[part] + here
            for j in range(i):
                off[part] = off[part] + block(i, j, part) * block(j, i, part)
    for part in range(2):
        diagonal[slot, part] = scaled * trace[part]
    total = scaled * ((own[0] - own[1]) + 2.0 * (off[0] - off[1]))

    @pl.when(slot == 0)
    def _():
        crossed[...] = total

    @pl.when(slot > 0)
    def _():
        crossed[...] += total

    @pl.when(slot == slots - 1)
    def _():
        held = diagonal.shape[0]
        cross_ref[...] = jnp.sum(crossed[...], axis=1, keepdims=True)
        shares, _, _, width = dense_ref.shape
        for t in range(TRANSFER_COUNT):
            keep = [(transfer_ref[s] == t).astype(jnp.int32).astype(F32) for s in range(held)]
            for part in range(2):
                value = keep[0] * diagonal[0, part]
                for s in range(1, held):
                    value = value + keep[s] * diagonal[s, part]
                low, high = t * vectors, (t + 1) * vectors
                for share in range(low // width, (high - 1) // width + 1):
                    first, last = max(low, share * width), min(high, (share + 1) * width)
                    dense_ref[share, part, :, first - share * width : last - share * width] = value[
                        :, first - low : last - low
                    ]


def on_diagonal(count):
    return lax.broadcasted_iota(jnp.int32, (count, count), 0) == lax.broadcasted_iota(jnp.int32, (count, count), 1)


def column_of(row):
    count = row.shape[1]
    return jnp.sum(jnp.where(on_diagonal(count), jnp.broadcast_to(row, (count, count)), 0.0), axis=1, keepdims=True)


def row_from(column):
    count = column.shape[0]
    return jnp.sum(jnp.where(on_diagonal(count), jnp.broadcast_to(column, (count, count)), 0.0), axis=0, keepdims=True)


def reduce_kernel(
    devices,
    groups,
    dense_ref,
    cross_ref,
    field_ref,
    weight_ref,
    bias_ref,
    total_ref,
    mean_ref,
    paired,
    summed,
    landed,
    own_sums,
    other_sums,
    own_mean,
    other_mean,
    pair_send,
    pair_recv,
    share_send,
    share_recv,
    sum_send,
    sum_recv,
    mean_send,
    mean_recv,
):
    me = lax.axis_index("pb")
    group = lax.axis_index("walk")
    walkers = weight_ref.shape[1]

    def pb_peer(step):
        return {"pb": lax.rem(me + step, devices)}

    def walk_peer(step):
        return {"walk": lax.rem(group + step, groups)}

    barrier = pltpu.get_barrier_semaphore()
    for step in range(1, devices):
        pl.semaphore_signal(barrier, inc=1, device_id=pb_peer(step), device_id_type=pl.DeviceIdType.MESH)
    for step in range(1, groups):
        pl.semaphore_signal(barrier, inc=1, device_id=walk_peer(step), device_id_type=pl.DeviceIdType.MESH)
    pl.semaphore_wait(barrier, devices + groups - 2)

    def send_all(source_of, target, send_sems, recv_sems, peer, count):
        copies = []
        for step in range(1, count):
            copy = pltpu.make_async_remote_copy(
                src_ref=source_of(step),
                dst_ref=target.at[step - 1],
                send_sem=send_sems.at[step - 1],
                recv_sem=recv_sems.at[step - 1],
                device_id=peer(step),
                device_id_type=pl.DeviceIdType.MESH,
            )
            copy.start()
            copies.append(copy)
        return copies

    parity, line = lax.rem(me, 2), me // 2
    lines = devices // 2
    order = [lines // 2] + [step for step in range(1, lines) if step != lines // 2] + [0]
    pairs = {}
    for step in order:
        target = lax.rem(line + step, lines)
        pairs[step] = pltpu.make_async_remote_copy(
            src_ref=dense_ref.at[2 * target + 1 - parity],
            dst_ref=paired.at[step],
            send_sem=pair_send.at[step],
            recv_sem=pair_recv.at[step],
            device_id={"pb": 2 * line + 1 - parity},
            device_id_type=pl.DeviceIdType.MESH,
        )
        pairs[step].start()
    shares = {}
    for step in order[:-1]:
        owner = 2 * lax.rem(line + step, lines) + parity
        pairs[step].wait_recv()
        summed[step - 1] = dense_ref[owner] + paired[step]
        shares[step] = pltpu.make_async_remote_copy(
            src_ref=summed.at[step - 1],
            dst_ref=landed.at[step - 1],
            send_sem=share_send.at[step - 1],
            recv_sem=share_recv.at[step - 1],
            device_id={"pb": owner},
            device_id_type=pl.DeviceIdType.MESH,
        )
        shares[step].start()
    weight = column_of(weight_ref[...])
    pairs[0].wait_recv()
    real = dense_ref[me, 0] + paired[0, 0]
    imag = dense_ref[me, 1] + paired[0, 1]
    for step in range(1, lines):
        shares[step].wait_recv()
        real = real + landed[step - 1, 0]
        imag = imag + landed[step - 1, 1]
    bias_ref[0] = real
    bias_ref[1] = imag
    shift_real = SQRT_STEP * real
    shift_imag = SQRT_STEP * imag
    field = field_ref[...]
    coulomb = 0.5 * jnp.sum(real * real - imag * imag, axis=1, keepdims=True)
    real_arg = jnp.sum(
        field * shift_real - 0.5 * (shift_real * shift_real - shift_imag * shift_imag), axis=1, keepdims=True
    )
    imag_arg = jnp.sum(field * shift_imag - shift_real * shift_imag, axis=1, keepdims=True)
    lane = lax.broadcasted_iota(jnp.int32, own_sums.shape, 1)
    energy_part = coulomb - 0.5 * cross_ref[...]
    packed = jnp.where(lane == 0, energy_part, jnp.where(lane == 1, real_arg, jnp.where(lane == 2, imag_arg, 0.0)))
    own_sums[...] = packed
    sums = send_all(lambda step: own_sums, other_sums, sum_send, sum_recv, pb_peer, devices)
    for step in range(1, devices):
        sums[step - 1].wait_recv()
    total = jnp.zeros_like(packed)
    for index in range(devices):
        step = lax.rem(me + devices - index, devices)
        arrived = other_sums[jnp.maximum(step - 1, 0)]
        total = total + jnp.where(step == 0, packed, arrived)
    total_ref[...] = total
    energy = jnp.sum(jnp.where(lane == 0, total, 0.0), axis=1, keepdims=True)
    weighted = jnp.sum(weight * energy, axis=0, keepdims=True)
    weights = jnp.sum(weight, axis=0, keepdims=True)
    lane = lax.broadcasted_iota(jnp.int32, own_mean.shape, 1)
    mean = jnp.where(lane == 0, weighted, jnp.where(lane == 1, weights, 0.0))
    own_mean[...] = mean
    means = send_all(lambda step: own_mean, other_mean, mean_send, mean_recv, walk_peer, groups)
    for step in range(1, groups):
        means[step - 1].wait_recv()
    total = jnp.zeros_like(mean)
    for index in range(groups):
        step = lax.rem(group + groups - index, groups)
        arrived = other_mean[jnp.maximum(step - 1, 0)]
        total = total + jnp.where(step == 0, mean, arrived)
    mean_ref[...] = total
    for copy in list(pairs.values()) + list(shares.values()) + sums + means:
        copy.wait_send()


def finish_kernel(sums_ref, total_ref, mean_ref, weight_ref, bias_ref, energy_ref, new_ref, mixed_ref):
    bias_ref[:, 0, :] = sums_ref[0]
    bias_ref[:, 1, :] = sums_ref[1]
    total = total_ref[...]
    weight = column_of(weight_ref[...])
    lane = lax.broadcasted_iota(jnp.int32, total.shape, 1)
    energy = jnp.sum(jnp.where(lane == 0, total, 0.0), axis=1, keepdims=True)
    real = jnp.sum(jnp.where(lane == 1, total, 0.0), axis=1, keepdims=True)
    imag = jnp.sum(jnp.where(lane == 2, total, 0.0), axis=1, keepdims=True)
    energy_ref[...] = row_from(energy)
    new_ref[...] = row_from(weight * jnp.exp(real) * jnp.maximum(jnp.cos(imag), 0.0))
    mean = mean_ref[:1, :]
    mixed_ref[...] = mean[:, 0:1] / mean[:, 1:2]


def local(greens, cholesky, slot_source, block_transfer_index, slot_multiplicity, fields, weight):
    devices = lax.axis_size("pb")
    groups = lax.axis_size("walk")
    me = lax.axis_index("pb")
    walkers, kpoints, flat = greens.shape
    slots, vectors, _ = cholesky.shape
    width = TRANSFER_COUNT * vectors // devices
    vmem = pl.BlockSpec(memory_space=pltpu.VMEM)
    smem = pl.BlockSpec(memory_space=pltpu.SMEM)

    outgoing = pl.pallas_call(
        functools.partial(select_kernel, devices),
        out_shape=(jax.ShapeDtypeStruct((walkers, flat), greens.dtype),) * slots,
        in_specs=[smem, vmem],
        out_specs=(vmem,) * slots,
        scratch_shapes=[pltpu.VMEM((walkers, kpoints, flat), F32), pltpu.VMEM((slots, walkers, flat), F32)],
        compiler_params=pltpu.CompilerParams(vmem_limit_bytes=VMEM_LIMIT),
        name="select",
    )(slot_source, greens)

    arrived = [outgoing[0]]
    for slot in range(1, slots):
        by = devices - offsets_of(devices)[slot]
        arrived.append(lax.ppermute(outgoing[slot], "pb", [(i, (i + by) % devices) for i in range(devices)]))

    rows = 2 * OCCUPIED_COUNT * walkers
    dense, cross = pl.pallas_call(
        compute_kernel,
        grid=(slots,),
        out_shape=(
            jax.ShapeDtypeStruct((devices, 2, walkers, width), F32),
            jax.ShapeDtypeStruct((walkers, 1), F32),
        ),
        in_specs=[
            smem,
            smem,
            pl.BlockSpec((1, vectors, flat), lambda s: (s, 0, 0)),
            pl.BlockSpec((2, WINDOW, 4 * WINDOW), lambda s: (0, 0, 0)),
        ]
        + [pl.BlockSpec((walkers, flat), lambda s: (0, 0))] * slots,
        out_specs=(
            pl.BlockSpec((devices, 2, walkers, width), lambda s: (0, 0, 0, 0)),
            pl.BlockSpec((walkers, 1), lambda s: (0, 0)),
        ),
        scratch_shapes=[
            pltpu.VMEM((2, rows, WINDOW), greens.dtype),
            pltpu.VMEM((OCCUPIED_COUNT, rows, vectors), F32),
            pltpu.VMEM((slots, 2, walkers, vectors), F32),
            pltpu.VMEM((walkers, vectors), F32),
            pltpu.VMEM((walkers, flat), greens.dtype),
        ],
        compiler_params=pltpu.CompilerParams(
            dimension_semantics=("arbitrary",), vmem_limit_bytes=VMEM_LIMIT
        ),
        name="terms",
    )(block_transfer_index, slot_multiplicity, cholesky, jnp.asarray(arrangement(), greens.dtype), *arrived)

    if width % vectors == 0:
        each = width // vectors
        field_share = lax.dynamic_slice_in_dim(fields, me * each, each, 1).reshape(walkers, width)
    else:
        flat_fields = fields.reshape(walkers, TRANSFER_COUNT * vectors)
        field_share = lax.dynamic_slice_in_dim(flat_fields, me * width, width, 1)

    sums, total, mean = pl.pallas_call(
        functools.partial(reduce_kernel, devices, groups),
        out_shape=(
            jax.ShapeDtypeStruct((2, walkers, width), F32),
            jax.ShapeDtypeStruct((walkers, 128), F32),
            jax.ShapeDtypeStruct((8, 128), F32),
        ),
        in_specs=[vmem] * 4,
        out_specs=(vmem,) * 3,
        scratch_shapes=[
            pltpu.VMEM((devices // 2, 2, walkers, width), F32),
            pltpu.VMEM((devices // 2 - 1, 2, walkers, width), F32),
            pltpu.VMEM((devices // 2 - 1, 2, walkers, width), F32),
            pltpu.VMEM((walkers, 128), F32),
            pltpu.VMEM((devices - 1, walkers, 128), F32),
            pltpu.VMEM((8, 128), F32),
            pltpu.VMEM((groups - 1, 8, 128), F32),
            pltpu.SemaphoreType.DMA((devices // 2,)),
            pltpu.SemaphoreType.DMA((devices // 2,)),
            pltpu.SemaphoreType.DMA((devices // 2 - 1,)),
            pltpu.SemaphoreType.DMA((devices // 2 - 1,)),
            pltpu.SemaphoreType.DMA((devices - 1,)),
            pltpu.SemaphoreType.DMA((devices - 1,)),
            pltpu.SemaphoreType.DMA((groups - 1,)),
            pltpu.SemaphoreType.DMA((groups - 1,)),
        ],
        compiler_params=pltpu.CompilerParams(collective_id=1, has_side_effects=True, vmem_limit_bytes=VMEM_LIMIT),
        name="reduce",
    )(dense, cross, field_share, weight.reshape(1, walkers))

    bias, energy, new_weight, mixed = pl.pallas_call(
        finish_kernel,
        out_shape=(
            jax.ShapeDtypeStruct((walkers, 2, width), F32),
            jax.ShapeDtypeStruct((1, walkers), F32),
            jax.ShapeDtypeStruct((1, walkers), F32),
            jax.ShapeDtypeStruct((1, 1), F32),
        ),
        in_specs=[vmem] * 4,
        out_specs=(vmem,) * 4,
        name="finish",
    )(sums, total, mean, weight.reshape(1, walkers))
    return (bias, energy.reshape(walkers), new_weight.reshape(walkers), mixed.reshape(()))


def solution(mesh):
    placed = (
        P("walk", "pb", None),
        P("pb", None, None),
        P(),
        P("pb"),
        P("pb"),
        P("walk", None, None),
        P("walk"),
    )
    return jax.shard_map(
        local,
        mesh=mesh,
        in_specs=placed,
        out_specs=(P("walk", None, "pb"), P("walk"), P("walk"), P()),
        check_vma=False,
    )
```

```python
import functools

import jax
import jax.numpy as jnp
import numpy as np
from jax import lax
from jax.experimental import pallas as pl
from jax.experimental.pallas import tpu as pltpu
from jax.sharding import PartitionSpec as P

ORBITAL_COUNT = 96
OCCUPIED_COUNT = 16
TRANSFER_COUNT = 16
SQRT_STEP = 0.05

DOUBLED = 2 * ORBITAL_COUNT
PAIR = 2 * DOUBLED
WINDOW = 256
SHIFT = PAIR - WINDOW
VMEM_LIMIT = 60 * 1024 * 1024
F32 = jnp.float32


def offsets_of(devices):
    return [0, devices - 1, 1, devices // 2]


def arrangement():
    table = np.zeros((2, WINDOW, 2, 2, WINDOW), np.float32)
    for parity in range(2):
        start = parity * (DOUBLED - SHIFT)
        for window in range(2):
            out = window * (DOUBLED - SHIFT)
            for q in range(ORBITAL_COUNT):
                re, im = start + q, start + ORBITAL_COUNT + q
                first, second = out + q, out + ORBITAL_COUNT + q
                table[parity, re, window, 0, first] = 1.0
                table[parity, im, window, 0, second] = -1.0
                table[parity, im, window, 1, first] = 1.0
                table[parity, re, window, 1, second] = 1.0
    return table.reshape(2, WINDOW, 4 * WINDOW)


def select_kernel(devices, source_ref, greens_ref, *rest):
    me = lax.axis_index("pb")
    walkers, kpoints, _ = greens_ref.shape
    outs, (wide, picked) = rest[:-2], rest[-2:]
    slots = len(outs)
    for w in range(walkers):
        wide[w] = greens_ref[w].astype(F32)
    for slot in range(slots):
        requester = lax.rem(me + devices - offsets_of(devices)[slot], devices)
        index = lax.rem(source_ref[requester * slots + slot], kpoints)
        for w in range(walkers):
            picked[slot, w : w + 1, :] = wide[w, pl.ds(index, 1), :]
        outs[slot][...] = picked[slot].astype(greens_ref.dtype)


def row_of(part, occupied, walkers):
    half = (OCCUPIED_COUNT // 2) * walkers
    return part * 2 * half + (occupied % 2) * half + (occupied // 2) * walkers


def compute_kernel(
    transfer_ref, multiple_ref, chol_ref, table_ref, *rest
):
    greens, (dense_ref, cross_ref, operand, product, diagonal, crossed, green) = rest[:-7], rest[-7:]
    slot = pl.program_id(0)
    slots = pl.num_programs(0)
    walkers = green.shape[0]
    vectors = chol_ref.shape[1]
    half = (OCCUPIED_COUNT // 2) * walkers
    pairs = OCCUPIED_COUNT // 2
    scaled = multiple_ref[slot].astype(F32)

    for index, green_ref in enumerate(greens):

        @pl.when(slot == index)
        def _():
            green[...] = green_ref[...]


    for parity in range(2):
        rows = jnp.concatenate(
            [green[:, PAIR * p + SHIFT * parity : PAIR * p + SHIFT * parity + WINDOW] for p in range(pairs)], 0
        )
        spread = jnp.dot(rows, table_ref[parity], preferred_element_type=F32).astype(operand.dtype)
        for window in range(2):
            for part in range(2):
                at = (window * 2 + part) * WINDOW
                operand[window, pl.ds(part * 2 * half + parity * half, half), :] = spread[:, at : at + WINDOW]

    def multiply(i):
        start = PAIR * (i // 2) + SHIFT * (i % 2)
        product[i] = lax.dot_general(
            operand[i % 2],
            chol_ref[0, :, start : start + WINDOW],
            (((1,), (1,)), ((), ())),
            preferred_element_type=F32,
        )

    def block(i, j, part):
        return product[i, pl.ds(row_of(part, j, walkers), walkers), :]

    zero = jnp.zeros((walkers, vectors), F32)
    off = [zero, zero]
    own = [zero, zero]
    trace = [zero, zero]
    multiply(0)
    for i in range(OCCUPIED_COUNT):
        if i + 1 < OCCUPIED_COUNT:
            multiply(i + 1)
        for part in range(2):
            here = block(i, i, part)
            own[part] = own[part] + here * here
            trace[part] = trace[part] + here
            for j in range(i):
                off[part] = off[part] + block(i, j, part) * block(j, i, part)
    for part in range(2):
        diagonal[slot, part] = scaled * trace[part]
    total = scaled * ((own[0] - own[1]) + 2.0 * (off[0] - off[1]))

    @pl.when(slot == 0)
    def _():
        crossed[...] = total

    @pl.when(slot > 0)
    def _():
        crossed[...] += total

    @pl.when(slot == slots - 1)
    def _():
        held = diagonal.shape[0]
        cross_ref[...] = jnp.sum(crossed[...], axis=1, keepdims=True)
        shares, _, _, width = dense_ref.shape
        for t in range(TRANSFER_COUNT):
            keep = [(transfer_ref[s] == t).astype(jnp.int32).astype(F32) for s in range(held)]
            for part in range(2):
                value = keep[0] * diagonal[0, part]
                for s in range(1, held):
                    value = value + keep[s] * diagonal[s, part]
                low, high = t * vectors, (t + 1) * vectors
                for share in range(low // width, (high - 1) // width + 1):
                    first, last = max(low, share * width), min(high, (share + 1) * width)
                    dense_ref[share, part, :, first - share * width : last - share * width] = value[
                        :, first - low : last - low
                    ]


def on_diagonal(count):
    return lax.broadcasted_iota(jnp.int32, (count, count), 0) == lax.broadcasted_iota(jnp.int32, (count, count), 1)


def column_of(row):
    count = row.shape[1]
    return jnp.sum(jnp.where(on_diagonal(count), jnp.broadcast_to(row, (count, count)), 0.0), axis=1, keepdims=True)


def row_from(column):
    count = column.shape[0]
    return jnp.sum(jnp.where(on_diagonal(count), jnp.broadcast_to(column, (count, count)), 0.0), axis=0, keepdims=True)


def reduce_kernel(
    devices,
    groups,
    dense_ref,
    cross_ref,
    field_ref,
    weight_ref,
    bias_ref,
    total_ref,
    mean_ref,
    paired,
    summed,
    landed,
    own_sums,
    other_sums,
    own_mean,
    other_mean,
    pair_send,
    pair_recv,
    share_send,
    share_recv,
    sum_send,
    sum_recv,
    mean_send,
    mean_recv,
):
    me = lax.axis_index("pb")
    group = lax.axis_index("walk")
    walkers = weight_ref.shape[1]

    def pb_peer(step):
        return {"pb": lax.rem(me + step, devices)}

    def walk_peer(step):
        return {"walk": lax.rem(group + step, groups)}

    barrier = pltpu.get_barrier_semaphore()
    for step in range(1, devices):
        pl.semaphore_signal(barrier, inc=1, device_id=pb_peer(step), device_id_type=pl.DeviceIdType.MESH)
    for step in range(1, groups):
        pl.semaphore_signal(barrier, inc=1, device_id=walk_peer(step), device_id_type=pl.DeviceIdType.MESH)
    pl.semaphore_wait(barrier, devices + groups - 2)

    def send_all(source_of, target, send_sems, recv_sems, peer, count):
        copies = []
        for step in range(1, count):
            copy = pltpu.make_async_remote_copy(
                src_ref=source_of(step),
                dst_ref=target.at[step - 1],
                send_sem=send_sems.at[step - 1],
                recv_sem=recv_sems.at[step - 1],
                device_id=peer(step),
                device_id_type=pl.DeviceIdType.MESH,
            )
            copy.start()
            copies.append(copy)
        return copies

    parity, line = lax.rem(me, 2), me // 2
    lines = devices // 2
    order = [lines // 2] + [step for step in range(1, lines) if step != lines // 2] + [0]
    pairs = {}
    for step in order:
        target = lax.rem(line + step, lines)
        pairs[step] = pltpu.make_async_remote_copy(
            src_ref=dense_ref.at[2 * target + 1 - parity],
            dst_ref=paired.at[step],
            send_sem=pair_send.at[step],
            recv_sem=pair_recv.at[step],
            device_id={"pb": 2 * line + 1 - parity},
            device_id_type=pl.DeviceIdType.MESH,
        )
        pairs[step].start()
    shares = {}
    for step in order[:-1]:
        owner = 2 * lax.rem(line + step, lines) + parity
        pairs[step].wait_recv()
        summed[step - 1] = dense_ref[owner] + paired[step]
        shares[step] = pltpu.make_async_remote_copy(
            src_ref=summed.at[step - 1],
            dst_ref=landed.at[step - 1],
            send_sem=share_send.at[step - 1],
            recv_sem=share_recv.at[step - 1],
            device_id={"pb": owner},
            device_id_type=pl.DeviceIdType.MESH,
        )
        shares[step].start()
    weight = column_of(weight_ref[...])
    pairs[0].wait_recv()
    real = dense_ref[me, 0] + paired[0, 0]
    imag = dense_ref[me, 1] + paired[0, 1]
    for step in range(1, lines):
        shares[step].wait_recv()
        real = real + landed[step - 1, 0]
        imag = imag + landed[step - 1, 1]
    bias_ref[0] = real
    bias_ref[1] = imag
    shift_real = SQRT_STEP * real
    shift_imag = SQRT_STEP * imag
    field = field_ref[...]
    coulomb = 0.5 * jnp.sum(real * real - imag * imag, axis=1, keepdims=True)
    real_arg = jnp.sum(
        field * shift_real - 0.5 * (shift_real * shift_real - shift_imag * shift_imag), axis=1, keepdims=True
    )
    imag_arg = jnp.sum(field * shift_imag - shift_real * shift_imag, axis=1, keepdims=True)
    lane = lax.broadcasted_iota(jnp.int32, own_sums.shape, 1)
    energy_part = coulomb - 0.5 * cross_ref[...]
    packed = jnp.where(lane == 0, energy_part, jnp.where(lane == 1, real_arg, jnp.where(lane == 2, imag_arg, 0.0)))
    own_sums[...] = packed
    sums = send_all(lambda step: own_sums, other_sums, sum_send, sum_recv, pb_peer, devices)
    for step in range(1, devices):
        sums[step - 1].wait_recv()
    total = jnp.zeros_like(packed)
    for index in range(devices):
        step = lax.rem(me + devices - index, devices)
        arrived = other_sums[jnp.maximum(step - 1, 0)]
        total = total + jnp.where(step == 0, packed, arrived)
    total_ref[...] = total
    energy = jnp.sum(jnp.where(lane == 0, total, 0.0), axis=1, keepdims=True)
    weighted = jnp.sum(weight * energy, axis=0, keepdims=True)
    weights = jnp.sum(weight, axis=0, keepdims=True)
    lane = lax.broadcasted_iota(jnp.int32, own_mean.shape, 1)
    mean = jnp.where(lane == 0, weighted, jnp.where(lane == 1, weights, 0.0))
    own_mean[...] = mean
    means = send_all(lambda step: own_mean, other_mean, mean_send, mean_recv, walk_peer, groups)
    for step in range(1, groups):
        means[step - 1].wait_recv()
    total = jnp.zeros_like(mean)
    for index in range(groups):
        step = lax.rem(group + groups - index, groups)
        arrived = other_mean[jnp.maximum(step - 1, 0)]
        total = total + jnp.where(step == 0, mean, arrived)
    mean_ref[...] = total
    for copy in list(pairs.values()) + list(shares.values()) + sums + means:
        copy.wait_send()


def finish_kernel(sums_ref, total_ref, mean_ref, weight_ref, bias_ref, energy_ref, new_ref, mixed_ref):
    bias_ref[:, 0, :] = sums_ref[0]
    bias_ref[:, 1, :] = sums_ref[1]
    total = total_ref[...]
    weight = column_of(weight_ref[...])
    lane = lax.broadcasted_iota(jnp.int32, total.shape, 1)
    energy = jnp.sum(jnp.where(lane == 0, total, 0.0), axis=1, keepdims=True)
    real = jnp.sum(jnp.where(lane == 1, total, 0.0), axis=1, keepdims=True)
    imag = jnp.sum(jnp.where(lane == 2, total, 0.0), axis=1, keepdims=True)
    energy_ref[...] = row_from(energy)
    new_ref[...] = row_from(weight * jnp.exp(real) * jnp.maximum(jnp.cos(imag), 0.0))
    mean = mean_ref[:1, :]
    mixed_ref[...] = mean[:, 0:1] / mean[:, 1:2]


def local(greens, cholesky, slot_source, block_transfer_index, slot_multiplicity, fields, weight):
    devices = lax.axis_size("pb")
    groups = lax.axis_size("walk")
    me = lax.axis_index("pb")
    walkers, kpoints, flat = greens.shape
    slots, vectors, _ = cholesky.shape
    width = TRANSFER_COUNT * vectors // devices
    vmem = pl.BlockSpec(memory_space=pltpu.VMEM)
    smem = pl.BlockSpec(memory_space=pltpu.SMEM)

    outgoing = pl.pallas_call(
        functools.partial(select_kernel, devices),
        out_shape=(jax.ShapeDtypeStruct((walkers, flat), greens.dtype),) * slots,
        in_specs=[smem, vmem],
        out_specs=(vmem,) * slots,
        scratch_shapes=[pltpu.VMEM((walkers, kpoints, flat), F32), pltpu.VMEM((slots, walkers, flat), F32)],
        compiler_params=pltpu.CompilerParams(vmem_limit_bytes=VMEM_LIMIT),
        name="select",
    )(slot_source, greens)

    arrived = [outgoing[0]]
    for slot in range(1, slots):
        by = devices - offsets_of(devices)[slot]
        arrived.append(lax.ppermute(outgoing[slot], "pb", [(i, (i + by) % devices) for i in range(devices)]))

    rows = 2 * OCCUPIED_COUNT * walkers
    dense, cross = pl.pallas_call(
        compute_kernel,
        grid=(slots,),
        out_shape=(
            jax.ShapeDtypeStruct((devices, 2, walkers, width), F32),
            jax.ShapeDtypeStruct((walkers, 1), F32),
        ),
        in_specs=[
            smem,
            smem,
            pl.BlockSpec((1, vectors, flat), lambda s: (s, 0, 0)),
            pl.BlockSpec((2, WINDOW, 4 * WINDOW), lambda s: (0, 0, 0)),
        ]
        + [pl.BlockSpec((walkers, flat), lambda s: (0, 0))] * slots,
        out_specs=(
            pl.BlockSpec((devices, 2, walkers, width), lambda s: (0, 0, 0, 0)),
            pl.BlockSpec((walkers, 1), lambda s: (0, 0)),
        ),
        scratch_shapes=[
            pltpu.VMEM((2, rows, WINDOW), greens.dtype),
            pltpu.VMEM((OCCUPIED_COUNT, rows, vectors), F32),
            pltpu.VMEM((slots, 2, walkers, vectors), F32),
            pltpu.VMEM((walkers, vectors), F32),
            pltpu.VMEM((walkers, flat), greens.dtype),
        ],
        compiler_params=pltpu.CompilerParams(
            dimension_semantics=("arbitrary",), vmem_limit_bytes=VMEM_LIMIT
        ),
        name="terms",
    )(block_transfer_index, slot_multiplicity, cholesky, jnp.asarray(arrangement(), greens.dtype), *arrived)

    if width % vectors == 0:
        each = width // vectors
        field_share = lax.dynamic_slice_in_dim(fields, me * each, each, 1).reshape(walkers, width)
    else:
        flat_fields = fields.reshape(walkers, TRANSFER_COUNT * vectors)
        field_share = lax.dynamic_slice_in_dim(flat_fields, me * width, width, 1)

    sums, total, mean = pl.pallas_call(
        functools.partial(reduce_kernel, devices, groups),
        out_shape=(
            jax.ShapeDtypeStruct((2, walkers, width), F32),
            jax.ShapeDtypeStruct((walkers, 128), F32),
            jax.ShapeDtypeStruct((8, 128), F32),
        ),
        in_specs=[vmem] * 4,
        out_specs=(vmem,) * 3,
        scratch_shapes=[
            pltpu.VMEM((devices // 2, 2, walkers, width), F32),
            pltpu.VMEM((devices // 2 - 1, 2, walkers, width), F32),
            pltpu.VMEM((devices // 2 - 1, 2, walkers, width), F32),
            pltpu.VMEM((walkers, 128), F32),
            pltpu.VMEM((devices - 1, walkers, 128), F32),
            pltpu.VMEM((8, 128), F32),
            pltpu.VMEM((groups - 1, 8, 128), F32),
            pltpu.SemaphoreType.DMA((devices // 2,)),
            pltpu.SemaphoreType.DMA((devices // 2,)),
            pltpu.SemaphoreType.DMA((devices // 2 - 1,)),
            pltpu.SemaphoreType.DMA((devices // 2 - 1,)),
            pltpu.SemaphoreType.DMA((devices - 1,)),
            pltpu.SemaphoreType.DMA((devices - 1,)),
            pltpu.SemaphoreType.DMA((groups - 1,)),
            pltpu.SemaphoreType.DMA((groups - 1,)),
        ],
        compiler_params=pltpu.CompilerParams(collective_id=1, has_side_effects=True, vmem_limit_bytes=VMEM_LIMIT),
        name="reduce",
    )(dense, cross, field_share, weight.reshape(1, walkers))

    bias, energy, new_weight, mixed = pl.pallas_call(
        finish_kernel,
        out_shape=(
            jax.ShapeDtypeStruct((walkers, 2, width), F32),
            jax.ShapeDtypeStruct((1, walkers), F32),
            jax.ShapeDtypeStruct((1, walkers), F32),
            jax.ShapeDtypeStruct((1, 1), F32),
        ),
        in_specs=[vmem] * 4,
        out_specs=(vmem,) * 4,
        name="finish",
    )(sums, total, mean, weight.reshape(1, walkers))
    return (bias, energy.reshape(walkers), new_weight.reshape(walkers), mixed.reshape(()))


def solution(mesh):
    placed = (
        P("walk", "pb", None),
        P("pb", None, None),
        P(),
        P("pb"),
        P("pb"),
        P("walk", None, None),
        P("walk"),
    )
    return jax.shard_map(
        local,
        mesh=mesh,
        in_specs=placed,
        out_specs=(P("walk", None, "pb"), P("walk"), P("walk"), P()),
        check_vma=False,
    )
```

```python
import functools

import jax
import jax.numpy as jnp
import numpy as np
from jax import lax
from jax.experimental import pallas as pl
from jax.experimental.pallas import tpu as pltpu
from jax.sharding import PartitionSpec as P

ORBITAL_COUNT = 96
OCCUPIED_COUNT = 16
TRANSFER_COUNT = 16
SQRT_STEP = 0.05

DOUBLED = 2 * ORBITAL_COUNT
PAIR = 2 * DOUBLED
WINDOW = 256
SHIFT = PAIR - WINDOW
LANES = 128
VMEM_LIMIT = 60 * 1024 * 1024
F32 = jnp.float32


def offsets_of(devices):
    return [0, devices - 1, 1, devices // 2]


def arrangement():
    table = np.zeros((2, WINDOW, 2, 2, WINDOW), np.float32)
    for parity in range(2):
        start = parity * (DOUBLED - SHIFT)
        for window in range(2):
            out = window * (DOUBLED - SHIFT)
            for q in range(ORBITAL_COUNT):
                re, im = start + q, start + ORBITAL_COUNT + q
                first, second = out + q, out + ORBITAL_COUNT + q
                table[parity, re, window, 0, first] = 1.0
                table[parity, im, window, 0, second] = -1.0
                table[parity, im, window, 1, first] = 1.0
                table[parity, re, window, 1, second] = 1.0
    return table.reshape(2, WINDOW, 4 * WINDOW)


def select_kernel(devices, source_ref, greens_ref, *rest):
    me = lax.axis_index("pb")
    walkers, kpoints, _ = greens_ref.shape
    outs, (wide, picked) = rest[:-2], rest[-2:]
    slots = len(outs)
    for w in range(walkers):
        wide[w] = greens_ref[w].astype(F32)
    for slot in range(slots):
        requester = lax.rem(me + devices - offsets_of(devices)[slot], devices)
        index = lax.rem(source_ref[requester * slots + slot], kpoints)
        for w in range(walkers):
            picked[slot, w : w + 1, :] = wide[w, pl.ds(index, 1), :]
        outs[slot][...] = picked[slot].astype(greens_ref.dtype)


def row_of(part, occupied, walkers):
    half = (OCCUPIED_COUNT // 2) * walkers
    return part * 2 * half + (occupied % 2) * half + (occupied // 2) * walkers


def compute_kernel(
    transfer_ref, multiple_ref, chol_ref, table_ref, *rest
):
    greens, (dense_ref, cross_ref, operand, product, diagonal, crossed, green, tails) = rest[:-8], rest[-8:]
    slot = pl.program_id(0)
    slots = pl.num_programs(0)
    walkers = green.shape[0]
    vectors = chol_ref.shape[1]
    half = (OCCUPIED_COUNT // 2) * walkers
    pairs = OCCUPIED_COUNT // 2
    scaled = multiple_ref[slot].astype(F32)

    for index, green_ref in enumerate(greens):

        @pl.when(slot == index)
        def _():
            green[...] = green_ref[...]


    for parity in range(2):
        rows = jnp.concatenate(
            [green[:, PAIR * p + SHIFT * parity : PAIR * p + SHIFT * parity + WINDOW] for p in range(pairs)], 0
        )
        spread = jnp.dot(rows, table_ref[parity], preferred_element_type=F32).astype(operand.dtype)
        for window in range(2):
            for part in range(2):
                at = (window * 2 + part) * WINDOW
                operand[window, pl.ds(part * 2 * half + parity * half, half), :] = spread[:, at : at + WINDOW]

    main = vectors // WINDOW * WINDOW
    rest_count = vectors - main

    @pl.when(slot == 0)
    def _():
        tails[...] = jnp.zeros_like(tails)

    def window_of(i):
        start = PAIR * (i // 2) + SHIFT * (i % 2)
        return slice(start, start + WINDOW)

    def times(parity, right):
        return lax.dot_general(operand[parity], right, (((1,), (1,)), ((), ())), preferred_element_type=F32)

    for i in range(OCCUPIED_COUNT):
        tails[i % 2, pl.ds(LANES * (i // 2), rest_count), :] = chol_ref[0, main:vectors, window_of(i)]
    for parity in range(2):
        ends = times(parity, tails[parity])
        for p in range(pairs):
            product[2 * p + parity, :, main : main + LANES] = ends[:, LANES * p : LANES * (p + 1)]

    def multiply(i):
        product[i, :, :main] = times(i % 2, chol_ref[0, :main, window_of(i)])

    def block(i, j, part):
        return product[i, pl.ds(row_of(part, j, walkers), walkers), :]

    zero = jnp.zeros((walkers, main + LANES), F32)
    off = [zero, zero]
    own = [zero, zero]
    trace = [zero, zero]
    multiply(0)
    for i in range(OCCUPIED_COUNT):
        if i + 1 < OCCUPIED_COUNT:
            multiply(i + 1)
        for part in range(2):
            here = block(i, i, part)
            own[part] = own[part] + here * here
            trace[part] = trace[part] + here
            for j in range(i):
                off[part] = off[part] + block(i, j, part) * block(j, i, part)
    for part in range(2):
        diagonal[slot, part] = scaled * trace[part][:, :vectors]
    total = scaled * ((own[0] - own[1]) + 2.0 * (off[0] - off[1]))[:, :vectors]

    @pl.when(slot == 0)
    def _():
        crossed[...] = total

    @pl.when(slot > 0)
    def _():
        crossed[...] += total

    @pl.when(slot == slots - 1)
    def _():
        held = diagonal.shape[0]
        cross_ref[...] = jnp.sum(crossed[...], axis=1, keepdims=True)
        shares, _, _, width = dense_ref.shape
        for t in range(TRANSFER_COUNT):
            keep = [(transfer_ref[s] == t).astype(jnp.int32).astype(F32) for s in range(held)]
            for part in range(2):
                value = keep[0] * diagonal[0, part]
                for s in range(1, held):
                    value = value + keep[s] * diagonal[s, part]
                low, high = t * vectors, (t + 1) * vectors
                for share in range(low // width, (high - 1) // width + 1):
                    first, last = max(low, share * width), min(high, (share + 1) * width)
                    dense_ref[share, part, :, first - share * width : last - share * width] = value[
                        :, first - low : last - low
                    ]


def on_diagonal(count):
    return lax.broadcasted_iota(jnp.int32, (count, count), 0) == lax.broadcasted_iota(jnp.int32, (count, count), 1)


def column_of(row):
    count = row.shape[1]
    return jnp.sum(jnp.where(on_diagonal(count), jnp.broadcast_to(row, (count, count)), 0.0), axis=1, keepdims=True)


def row_from(column):
    count = column.shape[0]
    return jnp.sum(jnp.where(on_diagonal(count), jnp.broadcast_to(column, (count, count)), 0.0), axis=0, keepdims=True)


def reduce_kernel(
    devices,
    groups,
    dense_ref,
    cross_ref,
    field_ref,
    weight_ref,
    bias_ref,
    total_ref,
    mean_ref,
    paired,
    summed,
    landed,
    own_sums,
    other_sums,
    own_mean,
    other_mean,
    pair_send,
    pair_recv,
    share_send,
    share_recv,
    sum_send,
    sum_recv,
    mean_send,
    mean_recv,
):
    me = lax.axis_index("pb")
    group = lax.axis_index("walk")
    walkers = weight_ref.shape[1]

    def pb_peer(step):
        return {"pb": lax.rem(me + step, devices)}

    def walk_peer(step):
        return {"walk": lax.rem(group + step, groups)}

    barrier = pltpu.get_barrier_semaphore()
    for step in range(1, devices):
        pl.semaphore_signal(barrier, inc=1, device_id=pb_peer(step), device_id_type=pl.DeviceIdType.MESH)
    for step in range(1, groups):
        pl.semaphore_signal(barrier, inc=1, device_id=walk_peer(step), device_id_type=pl.DeviceIdType.MESH)
    pl.semaphore_wait(barrier, devices + groups - 2)

    def send_all(source_of, target, send_sems, recv_sems, peer, count):
        copies = []
        for step in range(1, count):
            copy = pltpu.make_async_remote_copy(
                src_ref=source_of(step),
                dst_ref=target.at[step - 1],
                send_sem=send_sems.at[step - 1],
                recv_sem=recv_sems.at[step - 1],
                device_id=peer(step),
                device_id_type=pl.DeviceIdType.MESH,
            )
            copy.start()
            copies.append(copy)
        return copies

    parity, line = lax.rem(me, 2), me // 2
    lines = devices // 2
    order = [lines // 2] + [step for step in range(1, lines) if step != lines // 2] + [0]
    pairs = {}
    for step in order:
        target = lax.rem(line + step, lines)
        pairs[step] = pltpu.make_async_remote_copy(
            src_ref=dense_ref.at[2 * target + 1 - parity],
            dst_ref=paired.at[step],
            send_sem=pair_send.at[step],
            recv_sem=pair_recv.at[step],
            device_id={"pb": 2 * line + 1 - parity},
            device_id_type=pl.DeviceIdType.MESH,
        )
        pairs[step].start()
    shares = {}
    for step in order[:-1]:
        owner = 2 * lax.rem(line + step, lines) + parity
        pairs[step].wait_recv()
        summed[step - 1] = dense_ref[owner] + paired[step]
        shares[step] = pltpu.make_async_remote_copy(
            src_ref=summed.at[step - 1],
            dst_ref=landed.at[step - 1],
            send_sem=share_send.at[step - 1],
            recv_sem=share_recv.at[step - 1],
            device_id={"pb": owner},
            device_id_type=pl.DeviceIdType.MESH,
        )
        shares[step].start()
    weight = column_of(weight_ref[...])
    pairs[0].wait_recv()
    real = dense_ref[me, 0] + paired[0, 0]
    imag = dense_ref[me, 1] + paired[0, 1]
    for step in range(1, lines):
        shares[step].wait_recv()
        real = real + landed[step - 1, 0]
        imag = imag + landed[step - 1, 1]
    bias_ref[0] = real
    bias_ref[1] = imag
    shift_real = SQRT_STEP * real
    shift_imag = SQRT_STEP * imag
    field = field_ref[...]
    coulomb = 0.5 * jnp.sum(real * real - imag * imag, axis=1, keepdims=True)
    real_arg = jnp.sum(
        field * shift_real - 0.5 * (shift_real * shift_real - shift_imag * shift_imag), axis=1, keepdims=True
    )
    imag_arg = jnp.sum(field * shift_imag - shift_real * shift_imag, axis=1, keepdims=True)
    lane = lax.broadcasted_iota(jnp.int32, own_sums.shape, 1)
    energy_part = coulomb - 0.5 * cross_ref[...]
    packed = jnp.where(lane == 0, energy_part, jnp.where(lane == 1, real_arg, jnp.where(lane == 2, imag_arg, 0.0)))
    own_sums[...] = packed
    sums = send_all(lambda step: own_sums, other_sums, sum_send, sum_recv, pb_peer, devices)
    for step in range(1, devices):
        sums[step - 1].wait_recv()
    total = jnp.zeros_like(packed)
    for index in range(devices):
        step = lax.rem(me + devices - index, devices)
        arrived = other_sums[jnp.maximum(step - 1, 0)]
        total = total + jnp.where(step == 0, packed, arrived)
    total_ref[...] = total
    energy = jnp.sum(jnp.where(lane == 0, total, 0.0), axis=1, keepdims=True)
    weighted = jnp.sum(weight * energy, axis=0, keepdims=True)
    weights = jnp.sum(weight, axis=0, keepdims=True)
    lane = lax.broadcasted_iota(jnp.int32, own_mean.shape, 1)
    mean = jnp.where(lane == 0, weighted, jnp.where(lane == 1, weights, 0.0))
    own_mean[...] = mean
    means = send_all(lambda step: own_mean, other_mean, mean_send, mean_recv, walk_peer, groups)
    for step in range(1, groups):
        means[step - 1].wait_recv()
    total = jnp.zeros_like(mean)
    for index in range(groups):
        step = lax.rem(group + groups - index, groups)
        arrived = other_mean[jnp.maximum(step - 1, 0)]
        total = total + jnp.where(step == 0, mean, arrived)
    mean_ref[...] = total
    for copy in list(pairs.values()) + list(shares.values()) + sums + means:
        copy.wait_send()


def finish_kernel(sums_ref, total_ref, mean_ref, weight_ref, bias_ref, energy_ref, new_ref, mixed_ref):
    bias_ref[:, 0, :] = sums_ref[0]
    bias_ref[:, 1, :] = sums_ref[1]
    total = total_ref[...]
    weight = column_of(weight_ref[...])
    lane = lax.broadcasted_iota(jnp.int32, total.shape, 1)
    energy = jnp.sum(jnp.where(lane == 0, total, 0.0), axis=1, keepdims=True)
    real = jnp.sum(jnp.where(lane == 1, total, 0.0), axis=1, keepdims=True)
    imag = jnp.sum(jnp.where(lane == 2, total, 0.0), axis=1, keepdims=True)
    energy_ref[...] = row_from(energy)
    new_ref[...] = row_from(weight * jnp.exp(real) * jnp.maximum(jnp.cos(imag), 0.0))
    mean = mean_ref[:1, :]
    mixed_ref[...] = mean[:, 0:1] / mean[:, 1:2]


def local(greens, cholesky, slot_source, block_transfer_index, slot_multiplicity, fields, weight):
    devices = lax.axis_size("pb")
    groups = lax.axis_size("walk")
    me = lax.axis_index("pb")
    walkers, kpoints, flat = greens.shape
    slots, vectors, _ = cholesky.shape
    width = TRANSFER_COUNT * vectors // devices
    vmem = pl.BlockSpec(memory_space=pltpu.VMEM)
    smem = pl.BlockSpec(memory_space=pltpu.SMEM)

    outgoing = pl.pallas_call(
        functools.partial(select_kernel, devices),
        out_shape=(jax.ShapeDtypeStruct((walkers, flat), greens.dtype),) * slots,
        in_specs=[smem, vmem],
        out_specs=(vmem,) * slots,
        scratch_shapes=[pltpu.VMEM((walkers, kpoints, flat), F32), pltpu.VMEM((slots, walkers, flat), F32)],
        compiler_params=pltpu.CompilerParams(vmem_limit_bytes=VMEM_LIMIT),
        name="select",
    )(slot_source, greens)

    arrived = [outgoing[0]]
    for slot in range(1, slots):
        by = devices - offsets_of(devices)[slot]
        arrived.append(lax.ppermute(outgoing[slot], "pb", [(i, (i + by) % devices) for i in range(devices)]))

    rows = 2 * OCCUPIED_COUNT * walkers
    dense, cross = pl.pallas_call(
        compute_kernel,
        grid=(slots,),
        out_shape=(
            jax.ShapeDtypeStruct((devices, 2, walkers, width), F32),
            jax.ShapeDtypeStruct((walkers, 1), F32),
        ),
        in_specs=[
            smem,
            smem,
            pl.BlockSpec((1, vectors, flat), lambda s: (s, 0, 0)),
            pl.BlockSpec((2, WINDOW, 4 * WINDOW), lambda s: (0, 0, 0)),
        ]
        + [pl.BlockSpec((walkers, flat), lambda s: (0, 0))] * slots,
        out_specs=(
            pl.BlockSpec((devices, 2, walkers, width), lambda s: (0, 0, 0, 0)),
            pl.BlockSpec((walkers, 1), lambda s: (0, 0)),
        ),
        scratch_shapes=[
            pltpu.VMEM((2, rows, WINDOW), greens.dtype),
            pltpu.VMEM((OCCUPIED_COUNT, rows, vectors // WINDOW * WINDOW + LANES), F32),
            pltpu.VMEM((slots, 2, walkers, vectors), F32),
            pltpu.VMEM((walkers, vectors), F32),
            pltpu.VMEM((walkers, flat), greens.dtype),
            pltpu.VMEM((2, LANES * OCCUPIED_COUNT // 2, WINDOW), greens.dtype),
        ],
        compiler_params=pltpu.CompilerParams(
            dimension_semantics=("arbitrary",), vmem_limit_bytes=VMEM_LIMIT
        ),
        name="terms",
    )(block_transfer_index, slot_multiplicity, cholesky, jnp.asarray(arrangement(), greens.dtype), *arrived)

    if width % vectors == 0:
        each = width // vectors
        field_share = lax.dynamic_slice_in_dim(fields, me * each, each, 1).reshape(walkers, width)
    else:
        flat_fields = fields.reshape(walkers, TRANSFER_COUNT * vectors)
        field_share = lax.dynamic_slice_in_dim(flat_fields, me * width, width, 1)

    sums, total, mean = pl.pallas_call(
        functools.partial(reduce_kernel, devices, groups),
        out_shape=(
            jax.ShapeDtypeStruct((2, walkers, width), F32),
            jax.ShapeDtypeStruct((walkers, 128), F32),
            jax.ShapeDtypeStruct((8, 128), F32),
        ),
        in_specs=[vmem] * 4,
        out_specs=(vmem,) * 3,
        scratch_shapes=[
            pltpu.VMEM((devices // 2, 2, walkers, width), F32),
            pltpu.VMEM((devices // 2 - 1, 2, walkers, width), F32),
            pltpu.VMEM((devices // 2 - 1, 2, walkers, width), F32),
            pltpu.VMEM((walkers, 128), F32),
            pltpu.VMEM((devices - 1, walkers, 128), F32),
            pltpu.VMEM((8, 128), F32),
            pltpu.VMEM((groups - 1, 8, 128), F32),
            pltpu.SemaphoreType.DMA((devices // 2,)),
            pltpu.SemaphoreType.DMA((devices // 2,)),
            pltpu.SemaphoreType.DMA((devices // 2 - 1,)),
            pltpu.SemaphoreType.DMA((devices // 2 - 1,)),
            pltpu.SemaphoreType.DMA((devices - 1,)),
            pltpu.SemaphoreType.DMA((devices - 1,)),
            pltpu.SemaphoreType.DMA((groups - 1,)),
            pltpu.SemaphoreType.DMA((groups - 1,)),
        ],
        compiler_params=pltpu.CompilerParams(collective_id=1, has_side_effects=True, vmem_limit_bytes=VMEM_LIMIT),
        name="reduce",
    )(dense, cross, field_share, weight.reshape(1, walkers))

    bias, energy, new_weight, mixed = pl.pallas_call(
        finish_kernel,
        out_shape=(
            jax.ShapeDtypeStruct((walkers, 2, width), F32),
            jax.ShapeDtypeStruct((1, walkers), F32),
            jax.ShapeDtypeStruct((1, walkers), F32),
            jax.ShapeDtypeStruct((1, 1), F32),
        ),
        in_specs=[vmem] * 4,
        out_specs=(vmem,) * 4,
        name="finish",
    )(sums, total, mean, weight.reshape(1, walkers))
    return (bias, energy.reshape(walkers), new_weight.reshape(walkers), mixed.reshape(()))


def solution(mesh):
    placed = (
        P("walk", "pb", None),
        P("pb", None, None),
        P(),
        P("pb"),
        P("pb"),
        P("walk", None, None),
        P("walk"),
    )
    return jax.shard_map(
        local,
        mesh=mesh,
        in_specs=placed,
        out_specs=(P("walk", None, "pb"), P("walk"), P("walk"), P()),
        check_vma=False,
    )
```
